768 devices in a mesh: seq: 96 (over x, z, core), head: 8 (over y).
Axes of the slice: x: 4, y: 8, z: 12, core: 2. Of those that a mesh axis runs over, the one named last changes fastest.
Arguments:
- queries: bfloat16 [98304, 4096], P(('seq', 'head')), may hold values from -5 to 5
- keys: bfloat16 [98304, 1024], P(('seq', 'head')), may hold values from -5 to 5
- values: bfloat16 [98304, 1024], P(('seq', 'head')), may hold values from -6 to 6
- upstream: bfloat16 [98304, 4096], P('seq', 'head'), may hold values from -6 to 6
- lengths: int32 [96, 8], P('seq'), may hold values from 1 to 122, as said below
- guests: int32 [96, 8], P('seq'), may hold values from 0 to 1, as said below
- advantage: float32 [96, 8], P('seq'), may hold values from -4 to 4
- partner: int32 [96], replicated, may hold values from 0 to 95, as said below
Outputs:
- grad_q: bfloat16 [98304, 4096], P(('seq', 'head'))
- grad_k: bfloat16 [98304, 1024], P(('seq', 'head'))
- grad_v: bfloat16 [98304, 1024], P(('seq', 'head'))
The draws below stay inside these ranges and needn't reach their ends.
Inputs may be any that keep to these rules, and one draw needn't show every extreme that they name: `lengths`: every tree has a slot with a response of 122 tokens; rows of a slot beyond its length are padding. `guests`: every tree has at least one guest slot. The pairing is mutual and never pairs a tree with itself: partner[partner[i]] = i.
All inputs are finite; a program needn't handle non-finite values.
Results may differ from the reference program's by a relative error of at most 0.025.
Values may be sent and summed in bfloat16 or wider, within the bound.
No kernel may reach another device: no remote copies, remote signals or barrier semaphores. Data moves between devices by JAX's collectives and lax.ppermute only.
A program may use at most 64 MiB of HBM per device.

```python
import jax
import jax.numpy as jnp
from jax import lax

KV_HEADS = 8
HEAD_DIM = 128
D = 4096
PROMPT = 48
RESP = 8
RESP_LEN = 122
GROUP = 4
KV_WIDTH = 1024
ROWS = 1024
TREES = 96


def draw_queries(key, part):
    own_key = jax.random.fold_in(key, 1)
    array_shape = (TREES, ROWS, KV_HEADS, GROUP, HEAD_DIM)
    values_out = jnp.clip(jax.random.normal(own_key, array_shape), -5.0, 5.0)
    return values_out.reshape(TREES * ROWS, D).astype(jnp.bfloat16)


def draw_keys(key, part):
    own_key = jax.random.fold_in(key, 2)
    array_shape = (TREES, ROWS, KV_HEADS, HEAD_DIM)
    values_out = jnp.clip(jax.random.normal(own_key, array_shape), -5.0, 5.0)
    return values_out.reshape(TREES * ROWS, KV_WIDTH).astype(jnp.bfloat16)


def draw_lengths(key, part):
    first_key = jax.random.fold_in(key, 3)
    second_key = jax.random.fold_in(key, 4)
    drawn = jax.random.randint(first_key, (TREES, RESP), 1, RESP_LEN + 1)
    longest = jax.random.randint(second_key, (TREES,), 0, RESP)
    slot_index = jnp.arange(RESP)[None, :]
    return jnp.where(slot_index == longest[:, None], RESP_LEN, drawn).astype(jnp.int32)


def draw_guests(key, part):
    coins = jax.random.randint(jax.random.fold_in(key, 6), (TREES, RESP), 0, 2)
    forced = jax.random.randint(jax.random.fold_in(key, 7), (TREES,), 0, RESP)
    slot_index = jnp.arange(RESP)[None, :]
    return jnp.where(slot_index == forced[:, None], 1, coins).astype(jnp.int32)


def draw_partner(key, part):
    halfway = TREES // 2
    first_tree = jax.random.randint(jax.random.fold_in(key, 8), (), 0, halfway)
    second_tree = first_tree + halfway
    order = jax.random.permutation(jax.random.fold_in(key, 5), TREES).astype(jnp.int32)
    rank = jnp.zeros((TREES,), jnp.int32).at[order].set(jnp.arange(TREES, dtype=jnp.int32))
    index = jnp.arange(TREES, dtype=jnp.int32)
    scores = jnp.where(index == first_tree, -2, jnp.where(index == second_tree, -1, rank))
    arranged = jnp.argsort(scores, stable=True).astype(jnp.int32)
    left_trees = arranged[0::2]
    right_trees = arranged[1::2]
    paired = jnp.zeros((TREES,), jnp.int32)
    paired = paired.at[left_trees].set(right_trees)
    paired = paired.at[right_trees].set(left_trees)
    return paired


def level_of(rng, dims, cuts, low, top_value):
    gain = 1.0
    for position, parts in cuts:
        steps = jax.random.uniform(jax.random.fold_in(jax.random.fold_in(rng, 6), position), (parts,), jnp.float32, low / len(cuts), top_value / len(cuts))
        gain = gain * jnp.repeat(jnp.exp(steps), dims[position] // parts).reshape((-1,) + (1,) * (len(dims) - 1 - position))
    return gain


def gaussian(key, dims, width, bound, split=(), kind=jnp.bfloat16):
    entries = jax.random.normal(key, dims, jnp.float32) * width
    if len(split) > 0:
        entries = level_of(key, dims, split, -0.22, 0.18) * entries
    return jnp.clip(entries, min=-bound, max=bound).astype(kind)


def setup_inputs(seed: int = 0) -> dict:
    streams_of = jax.random.split(jax.random.key(seed), 9)
    return {
        "queries": draw_queries(jax.random.fold_in(streams_of[8], 71), 0),
        "keys": draw_keys(jax.random.fold_in(streams_of[8], 71), 0),
        "values": gaussian(streams_of[2], (TREES * ROWS, KV_WIDTH), 1.0, 6.0, ((0, 768),)),
        "upstream": gaussian(streams_of[3], (TREES * ROWS, D), 1.0, 6.0, ((0, 96), (1, 8))),
        "lengths": draw_lengths(jax.random.fold_in(streams_of[8], 71), 0),
        "guests": draw_guests(jax.random.fold_in(streams_of[8], 71), 0),
        "advantage": gaussian(streams_of[6], (TREES, RESP), 1.0, 4.0, ((0, 96),), jnp.float32),
        "partner": draw_partner(jax.random.fold_in(streams_of[8], 71), 0),
    }


def product(form, left, right):
    return jnp.einsum(form, left.astype(jnp.float32), right.astype(jnp.float32))


def forward_block(q_blk, key_blk, val_blk, allowed):
    scaling = q_blk.shape[-1] ** -0.5
    scores = product('blhgd,bkhd->bhglk', q_blk, key_blk) * scaling
    scores = jnp.where(allowed, scores, -jnp.inf)
    highest = jnp.max(scores, axis=-1, keepdims=True)
    lifted = jnp.exp(scores - highest)
    prob_full = lifted / jnp.sum(lifted, axis=-1, keepdims=True)
    prob_low = lax.optimization_barrier(prob_full.astype(jnp.bfloat16))
    output = product('bhglk,bkhd->blhgd', prob_low, val_blk)
    return prob_full, prob_low, output


def backward_block(prob_full, prob_low, output, q_blk, key_blk, val_blk, cot_blk):
    scaling = q_blk.shape[-1] ** -0.5
    grad_val = product('bhglk,blhgd->bkhd', prob_low, cot_blk)
    grad_prob = product('blhgd,bkhd->bhglk', cot_blk, val_blk)
    row_inner = jnp.sum(cot_blk.astype(jnp.float32) * output, axis=-1)
    row_inner = jnp.transpose(row_inner, (0, 2, 3, 1))[..., None]
    grad_score = prob_full * (grad_prob - row_inner) * scaling
    score_low = lax.optimization_barrier(grad_score.astype(jnp.bfloat16))
    grad_query = product('bhglk,bkhd->blhgd', score_low, key_blk)
    grad_key = product('bhglk,blhgd->bkhd', score_low, q_blk)
    return grad_query, grad_key, grad_val


def tree_pass(q_tree, k_tree, v_tree, far_keys, far_vals, cot_tree, lens_tree, guest_tree, adv_tree):
    heads_kv = k_tree.shape[1]
    group_size = q_tree.shape[2]
    head_width = q_tree.shape[3]
    slot_rows = jnp.arange(RESP_LEN, dtype=jnp.int32)
    valid_slot = (slot_rows[None, :] < lens_tree[:, None]).astype(jnp.float32)
    weighting = valid_slot * adv_tree[:, None]
    cot_slot = cot_tree[PROMPT:].astype(jnp.float32).reshape(RESP, RESP_LEN, heads_kv, group_size, head_width)
    cot_slot = lax.optimization_barrier((cot_slot * weighting[:, :, None, None, None]).astype(jnp.bfloat16))
    q_prompt = q_tree[:PROMPT][None]
    k_prompt = k_tree[:PROMPT][None]
    v_prompt = v_tree[:PROMPT][None]
    prompt_rows = jnp.arange(PROMPT, dtype=jnp.int32)
    causal = prompt_rows[:, None] >= prompt_rows[None, :]
    prob_full, prob_low, out_prompt = forward_block(q_prompt, k_prompt, v_prompt, causal)
    dq_prompt, dk_prompt, dv_prompt = backward_block(prob_full, prob_low, out_prompt, q_prompt, k_prompt, v_prompt, cot_tree[:PROMPT][None])
    chosen = (guest_tree == 1)[:, None, None, None]
    pre_keys = jnp.where(chosen, far_keys[None], k_tree[:PROMPT][None])
    pre_vals = jnp.where(chosen, far_vals[None], v_tree[:PROMPT][None])
    keys_slot = jnp.concatenate([pre_keys, k_tree[PROMPT:].reshape(RESP, RESP_LEN, heads_kv, head_width)], axis=1)
    vals_slot = jnp.concatenate([pre_vals, v_tree[PROMPT:].reshape(RESP, RESP_LEN, heads_kv, head_width)], axis=1)
    columns = jnp.arange(PROMPT + RESP_LEN, dtype=jnp.int32)
    allowed = (columns[None, :] < PROMPT) | (columns[None, :] - PROMPT <= slot_rows[:, None])
    q_slot = q_tree[PROMPT:].reshape(RESP, RESP_LEN, heads_kv, group_size, head_width)
    prob_full, prob_low, out_slot = forward_block(q_slot, keys_slot, vals_slot, allowed)
    out_slot = out_slot * valid_slot[:, :, None, None, None]
    dq_slot, dk_slot, dv_slot = backward_block(prob_full, prob_low, out_slot, q_slot, keys_slot, vals_slot, cot_slot)
    guest_f = guest_tree.astype(jnp.float32)[:, None, None, None]
    own_dk = dk_prompt[0] + jnp.sum((1.0 - guest_f) * dk_slot[:, :PROMPT], axis=0)
    own_dv = dv_prompt[0] + jnp.sum((1.0 - guest_f) * dv_slot[:, :PROMPT], axis=0)
    far_dk = jnp.sum(guest_f * dk_slot[:, :PROMPT], axis=0)
    far_dv = jnp.sum(guest_f * dv_slot[:, :PROMPT], axis=0)
    grad_k = jnp.concatenate([own_dk, dk_slot[:, PROMPT:].reshape(RESP * RESP_LEN, heads_kv, head_width)], axis=0)
    grad_v = jnp.concatenate([own_dv, dv_slot[:, PROMPT:].reshape(RESP * RESP_LEN, heads_kv, head_width)], axis=0)
    grad_q = jnp.concatenate([dq_prompt[0], dq_slot.reshape(RESP * RESP_LEN, heads_kv, group_size, head_width)], axis=0)
    return grad_q, grad_k, grad_v, far_dk, far_dv


def reference(queries, keys, values, upstream, lengths, guests, advantage, partner):
    q_all = queries.reshape(TREES, ROWS, KV_HEADS, GROUP, HEAD_DIM)
    k_all = keys.reshape(TREES, ROWS, KV_HEADS, HEAD_DIM)
    v_all = values.reshape(TREES, ROWS, KV_HEADS, HEAD_DIM)
    cot_all = upstream.reshape(TREES, ROWS, KV_HEADS, GROUP, HEAD_DIM)
    far_keys = k_all[partner, :PROMPT]
    far_vals = v_all[partner, :PROMPT]

    def one_tree(items):
        return tree_pass(*items)

    grad_q, grad_k, grad_v, far_dk, far_dv = lax.map(one_tree, (q_all, k_all, v_all, far_keys, far_vals, cot_all, lengths, guests, advantage))
    grad_k = grad_k.at[:, :PROMPT].add(far_dk[partner])
    grad_v = grad_v.at[:, :PROMPT].add(far_dv[partner])
    return (grad_q.astype(jnp.bfloat16).reshape(TREES * ROWS, D), grad_k.astype(jnp.bfloat16).reshape(TREES * ROWS, KV_WIDTH), grad_v.astype(jnp.bfloat16).reshape(TREES * ROWS, KV_WIDTH))
```

```python
import jax
import jax.numpy as jnp
from jax import lax
from jax.experimental import pallas as pl
from jax.experimental.pallas import tpu as pltpu
from jax.sharding import Mesh, PartitionSpec as P

HEAD_DIM = 128
PROMPT = 48
RESP = 8
RESP_LEN = 122
ROWS = 1024
GROUP = 4
KV_HEADS = 8
WINDOW = 128
TREES = ("x", "z", "core")
PLANE = ("x", "core")
X, Z, CORE = 4, 12, 2


def attend(q_rows, keys, vals, cot, allowed):
    scaling = HEAD_DIM ** (-0.5)
    nt = (((1,), (1,)), ((), ()))
    scores = lax.dot_general(keys, q_rows, nt, preferred_element_type=jnp.float32) * scaling
    scores = jnp.where(allowed, scores, -jnp.inf)
    lifted = jnp.exp(scores - jnp.max(scores, axis=0, keepdims=True))
    probs = lifted * (1.0 / jnp.sum(lifted, axis=0, keepdims=True))
    probs_low = probs.astype(jnp.bfloat16)
    grad_probs = lax.dot_general(vals, cot, nt, preferred_element_type=jnp.float32)
    inner = jnp.sum(probs_low.astype(jnp.float32) * grad_probs, axis=0, keepdims=True)
    grad_scores = (probs * (grad_probs - inner) * scaling).astype(jnp.bfloat16)
    grad_v = jnp.dot(probs_low, cot, preferred_element_type=jnp.float32)
    grad_k = jnp.dot(grad_scores, q_rows, preferred_element_type=jnp.float32)
    tn = (((0,), (0,)), ((), ()))
    grad_q = lax.dot_general(grad_scores, keys, tn, preferred_element_type=jnp.float32)
    return grad_q, jnp.concatenate([grad_k, grad_v], axis=1)


def stack_heads(block):
    return jnp.concatenate(
        [block[:, j * HEAD_DIM : (j + 1) * HEAD_DIM] for j in range(GROUP)], axis=0
    )


def unstack_heads(block, rows):
    return jnp.concatenate([block[j * rows : (j + 1) * rows] for j in range(GROUP)], axis=1)


def attention_kernel(ints, adv, q_ref, kv_ref, cot_ref, far_in, gq_ref, gkv_ref, far_out, own_out, pre, acc):
    iota = lax.broadcasted_iota
    pre[0] = kv_ref[:PROMPT, :]
    pre[1] = far_in[ints[2 * RESP]]
    acc[1] = jnp.zeros((PROMPT, 2 * HEAD_DIM), jnp.float32)

    wide = (PROMPT, GROUP * PROMPT)
    query = iota(jnp.int32, wide, 1)
    for j in range(1, GROUP):
        query = jnp.where(query >= PROMPT, query - PROMPT, query)
    grad_q, grad_kv = attend(
        stack_heads(q_ref[:PROMPT, :]),
        pre[0, :, :HEAD_DIM],
        pre[0, :, HEAD_DIM:],
        stack_heads(cot_ref[:PROMPT, :]),
        iota(jnp.int32, wide, 0) <= query,
    )
    gq_ref[:PROMPT, :] = unstack_heads(grad_q, PROMPT).astype(jnp.bfloat16)
    gkv_ref[:PROMPT, :] = jnp.zeros((PROMPT, 2 * HEAD_DIM), jnp.bfloat16)
    acc[0] = grad_kv

    for slot in range(RESP):
        first = PROMPT + RESP_LEN * slot
        start = first // 8 * 8
        skip = first - start
        rows = slice(start, start + WINDOW)
        guest = ints[RESP + slot]
        keys = jnp.concatenate([pre[guest, :, :HEAD_DIM], kv_ref[rows, :HEAD_DIM]], axis=0)
        vals = jnp.concatenate([pre[guest, :, HEAD_DIM:], kv_ref[rows, HEAD_DIM:]], axis=0)
        token = iota(jnp.int32, (WINDOW, GROUP * HEAD_DIM), 0) - skip
        weight = jnp.where((token >= 0) & (token < ints[slot]), adv[slot], 0.0)
        cot = (cot_ref[rows, :].astype(jnp.float32) * weight).astype(jnp.bfloat16)
        shape = (PROMPT + WINDOW, GROUP * WINDOW)
        key = iota(jnp.int32, shape, 0)
        query = iota(jnp.int32, shape, 1) & (WINDOW - 1)
        allowed = (key < PROMPT) | ((key >= PROMPT + skip) & (key - PROMPT <= query))
        grad_q, grad_kv = attend(stack_heads(q_ref[rows, :]), keys, vals, stack_heads(cot), allowed)
        acc[guest] += grad_kv[:PROMPT]
        for ref, new in ((gq_ref, unstack_heads(grad_q, WINDOW)), (gkv_ref, grad_kv[PROMPT:])):
            if skip:
                old = ref[start : start + 8, :].astype(jnp.float32)
                top = jnp.where(iota(jnp.int32, old.shape, 0) < skip, old, new[:8])
                new = jnp.concatenate([top, new[8:]], axis=0)
            ref[rows, :] = new.astype(jnp.bfloat16)

    own_out[...] = acc[0]
    far = acc[1].astype(jnp.bfloat16)
    for i in range(X * CORE):
        far_out[i] = far


def attention(ints, adv, q_heads, kv_heads, cot, far):
    vmem = pl.BlockSpec(memory_space=pltpu.VMEM)
    smem = pl.BlockSpec(memory_space=pltpu.SMEM)
    width = 2 * HEAD_DIM
    return pl.pallas_call(
        attention_kernel,
        out_shape=(
            jax.ShapeDtypeStruct((ROWS, GROUP * HEAD_DIM), jnp.bfloat16),
            jax.ShapeDtypeStruct((ROWS, width), jnp.bfloat16),
            jax.ShapeDtypeStruct((X * CORE, PROMPT, width), jnp.bfloat16),
            jax.ShapeDtypeStruct((PROMPT, width), jnp.float32),
        ),
        in_specs=[smem, smem, vmem, vmem, vmem, vmem],
        out_specs=(vmem, vmem, vmem, vmem),
        scratch_shapes=[
            pltpu.VMEM((2, PROMPT, width), jnp.bfloat16),
            pltpu.VMEM((2, PROMPT, width), jnp.float32),
        ],
        cost_estimate=pl.CostEstimate(flops=10**9, transcendentals=720896, bytes_accessed=5 * 2**20),
        name="attention",
    )(ints, adv, q_heads, kv_heads, cot, far)


def pick_kernel(index, blocks, out):
    for i in range(Z):
        out[i] = blocks[index[i]]


def pick(index, blocks):
    return pl.pallas_call(
        pick_kernel,
        out_shape=jax.ShapeDtypeStruct((Z,) + blocks.shape[1:], blocks.dtype),
        in_specs=[pl.BlockSpec(memory_space=pltpu.SMEM), pl.BlockSpec(memory_space=pltpu.VMEM)],
        out_specs=pl.BlockSpec(memory_space=pltpu.VMEM),
        cost_estimate=pl.CostEstimate(flops=0, transcendentals=0, bytes_accessed=2**19),
        name="pick",
    )(index, blocks)


def exchange(copies, route):
    plane = lax.all_to_all(copies, PLANE, split_axis=0, concat_axis=0, tiled=True)
    return lax.all_to_all(pick(route, plane), "z", split_axis=0, concat_axis=0, tiled=True)


def local(queries, keys, values, upstream, lengths, guests, advantage, partner):
    rows = queries.shape[0]

    def by_head(array):
        return array.reshape(rows, KV_HEADS, -1).transpose(1, 0, 2)

    kv = jnp.concatenate([by_head(keys), by_head(values)], axis=2)
    kv = lax.all_to_all(kv, "head", split_axis=0, concat_axis=0, tiled=True).reshape(ROWS, -1)
    q = lax.all_to_all(by_head(queries), "head", split_axis=0, concat_axis=0, tiled=True)

    x, z, core = (lax.axis_index(name) for name in TREES)
    mate = partner[(x * Z + z) * CORE + core]
    column = partner[(x * Z + jnp.arange(Z)) * CORE + core]
    route = column // (Z * CORE) * CORE + column % CORE
    ints = jnp.concatenate([lengths[0], guests[0], (mate // CORE % Z)[None]]).astype(jnp.int32)

    copies = jnp.broadcast_to(kv[None, :PROMPT], (X * CORE, PROMPT, 2 * HEAD_DIM))
    far = exchange(copies, route)
    grad_q, grad_kv, far_copies, own = attention(
        ints, advantage[0], q.reshape(ROWS, -1), kv, upstream, far
    )
    back = exchange(far_copies, route)
    back = lax.dynamic_index_in_dim(back, ints[2 * RESP], 0, keepdims=False)
    prompt = (own + back.astype(jnp.float32)).astype(jnp.bfloat16)
    grad_kv = jnp.concatenate([prompt, grad_kv[PROMPT:]], axis=0)

    def by_row(array):
        array = lax.all_to_all(
            array.reshape(KV_HEADS, rows, -1), "head", split_axis=0, concat_axis=0, tiled=True
        )
        return array.transpose(1, 0, 2)

    grad_q = by_row(grad_q).reshape(rows, -1)
    grad_kv = by_row(grad_kv)
    return (
        grad_q,
        grad_kv[:, :, :HEAD_DIM].reshape(rows, -1),
        grad_kv[:, :, HEAD_DIM:].reshape(rows, -1),
    )


def solution(mesh):
    mesh = Mesh(mesh.devices.reshape(X, Z, CORE, KV_HEADS), TREES + ("head",))
    tokens = P(TREES + ("head",), None)
    trees = P(TREES, None)
    return jax.shard_map(
        local,
        mesh=mesh,
        in_specs=(tokens, tokens, tokens, P(TREES, "head"), trees, trees, trees, P()),
        out_specs=(tokens, tokens, tokens),
        check_vma=False,
    )
```

```python
import jax
import jax.numpy as jnp
from jax import lax
from jax.experimental import pallas as pl
from jax.experimental.pallas import tpu as pltpu
from jax.sharding import Mesh, PartitionSpec as P

HEAD_DIM = 128
PROMPT = 48
RESP = 8
RESP_LEN = 122
ROWS = 1024
GROUP = 4
KV_HEADS = 8
WINDOW = 128
Q = GROUP * HEAD_DIM
KV = 2 * HEAD_DIM
TREES = ("x", "z", "core")
PLANE = ("x", "core")
X, Z, CORE = 4, 12, 2


def attend(q_rows, keys, vals, cot, allowed):
    scaling = HEAD_DIM ** (-0.5)
    nt = (((1,), (1,)), ((), ()))
    scores = lax.dot_general(keys, q_rows, nt, preferred_element_type=jnp.float32) * scaling
    scores = jnp.where(allowed, scores, -jnp.inf)
    lifted = jnp.exp(scores - jnp.max(scores, axis=0, keepdims=True))
    probs = lifted * (1.0 / jnp.sum(lifted, axis=0, keepdims=True))
    probs_low = probs.astype(jnp.bfloat16)
    grad_probs = lax.dot_general(vals, cot, nt, preferred_element_type=jnp.float32)
    inner = jnp.sum(probs_low.astype(jnp.float32) * grad_probs, axis=0, keepdims=True)
    grad_scores = (probs * (grad_probs - inner) * scaling).astype(jnp.bfloat16)
    grad_v = jnp.dot(probs_low, cot, preferred_element_type=jnp.float32)
    grad_k = jnp.dot(grad_scores, q_rows, preferred_element_type=jnp.float32)
    tn = (((0,), (0,)), ((), ()))
    grad_q = lax.dot_general(grad_scores, keys, tn, preferred_element_type=jnp.float32)
    return grad_q, jnp.concatenate([grad_k, grad_v], axis=1)


def stack_heads(block):
    return jnp.concatenate(
        [block[:, j * HEAD_DIM : (j + 1) * HEAD_DIM] for j in range(GROUP)], axis=0
    )


def unstack_heads(block, rows):
    return jnp.concatenate([block[j * rows : (j + 1) * rows] for j in range(GROUP)], axis=1)


def attention_kernel(ints, adv, qkv, prompt, cot_ref, stay, cross, grads, far_out, own_out, pre, acc):
    iota = lax.broadcasted_iota
    pre[0] = prompt[...]
    for crossed, ref in enumerate((stay, cross)):

        @pl.when(ints[2 * RESP] == crossed)
        def _():
            pre[1] = ref[...]

    acc[1] = jnp.zeros((PROMPT, KV), jnp.float32)

    wide = (PROMPT, GROUP * PROMPT)
    query = iota(jnp.int32, wide, 1)
    for j in range(1, GROUP):
        query = jnp.where(query >= PROMPT, query - PROMPT, query)
    grad_q, grad_kv = attend(
        stack_heads(qkv[:PROMPT, :Q]),
        pre[0, :, :HEAD_DIM],
        pre[0, :, HEAD_DIM:],
        stack_heads(cot_ref[:PROMPT, :]),
        iota(jnp.int32, wide, 0) <= query,
    )
    grads[:PROMPT, :Q] = unstack_heads(grad_q, PROMPT).astype(jnp.bfloat16)
    grads[:PROMPT, Q:] = jnp.zeros((PROMPT, KV), jnp.bfloat16)
    acc[0] = grad_kv

    for slot in range(RESP):
        first = PROMPT + RESP_LEN * slot
        start = first // 8 * 8
        skip = first - start
        rows = slice(start, start + WINDOW)
        guest = ints[RESP + slot]
        keys = jnp.concatenate([pre[guest, :, :HEAD_DIM], qkv[rows, Q : Q + HEAD_DIM]], axis=0)
        vals = jnp.concatenate([pre[guest, :, HEAD_DIM:], qkv[rows, Q + HEAD_DIM :]], axis=0)
        token = iota(jnp.int32, (WINDOW, Q), 0) - skip
        weight = jnp.where((token >= 0) & (token < ints[slot]), adv[slot], 0.0)
        cot = (cot_ref[rows, :].astype(jnp.float32) * weight).astype(jnp.bfloat16)
        shape = (PROMPT + WINDOW, GROUP * WINDOW)
        key = iota(jnp.int32, shape, 0)
        query = iota(jnp.int32, shape, 1) & (WINDOW - 1)
        allowed = (key < PROMPT) | ((key >= PROMPT + skip) & (key - PROMPT <= query))
        grad_q, grad_kv = attend(stack_heads(qkv[rows, :Q]), keys, vals, stack_heads(cot), allowed)
        acc[guest] += grad_kv[:PROMPT]
        new = jnp.concatenate([unstack_heads(grad_q, WINDOW), grad_kv[PROMPT:]], axis=1)
        if skip:
            old = grads[start : start + 8, :].astype(jnp.float32)
            top = jnp.where(iota(jnp.int32, old.shape, 0) < skip, old, new[:8])
            new = jnp.concatenate([top, new[8:]], axis=0)
        grads[rows, :] = new.astype(jnp.bfloat16)

    own_out[...] = acc[0]
    far_out[...] = acc[1].astype(jnp.bfloat16)


VMEM = pl.BlockSpec(memory_space=pltpu.VMEM)
SMEM = pl.BlockSpec(memory_space=pltpu.SMEM)


def attention(ints, adv, qkv, prompt, cot, stay, cross):
    return pl.pallas_call(
        attention_kernel,
        out_shape=(
            jax.ShapeDtypeStruct((ROWS, Q + KV), jnp.bfloat16),
            jax.ShapeDtypeStruct((PROMPT, KV), jnp.bfloat16),
            jax.ShapeDtypeStruct((PROMPT, KV), jnp.float32),
        ),
        in_specs=[SMEM] * 2 + [VMEM] * 5,
        out_specs=(VMEM, VMEM, VMEM),
        scratch_shapes=[
            pltpu.VMEM((2, PROMPT, KV), jnp.bfloat16),
            pltpu.VMEM((2, PROMPT, KV), jnp.float32),
        ],
        cost_estimate=pl.CostEstimate(flops=10**9, transcendentals=720896, bytes_accessed=5 * 2**20),
        name="attention",
    )(ints, adv, qkv, prompt, cot, stay, cross)


def spread_kernel(index, blocks, *outs):
    for k, out in enumerate(outs):
        for i in range(CORE):
            out[i] = blocks[index[CORE * k + i]]


def spread(index, blocks):
    pair = jax.ShapeDtypeStruct((CORE,) + blocks.shape[1:], blocks.dtype)
    return pl.pallas_call(
        spread_kernel,
        out_shape=(pair,) * X,
        in_specs=[SMEM, VMEM],
        out_specs=(VMEM,) * X,
        cost_estimate=pl.CostEstimate(flops=0, transcendentals=0, bytes_accessed=2**19),
        name="spread",
    )(index, blocks)


def narrow_kernel(index, *refs):
    pairs, outs = refs[:X], refs[X:]
    for i, out in enumerate(outs):
        for k, pair in enumerate(pairs):

            @pl.when(index[i] == k)
            def _():
                out[...] = pair[index[CORE + i]]


def narrow(index, pairs):
    block = jax.ShapeDtypeStruct(pairs[0].shape[1:], pairs[0].dtype)
    return pl.pallas_call(
        narrow_kernel,
        out_shape=(block,) * CORE,
        in_specs=[SMEM] + [VMEM] * X,
        out_specs=(VMEM,) * CORE,
        cost_estimate=pl.CostEstimate(flops=0, transcendentals=0, bytes_accessed=2**18),
        name="narrow",
    )(index, *pairs)


def exchange(block, to_x, to_core):
    pairs = spread(to_x, lax.all_gather(block, "z"))
    pairs = [pairs[0]] + [
        lax.ppermute(pairs[k], "x", [(i, (i + k) % X) for i in range(X)]) for k in range(1, X)
    ]
    stay, leave = narrow(to_core, pairs)
    return stay, lax.ppermute(leave, "core", [(0, 1), (1, 0)])


def local(queries, keys, values, upstream, lengths, guests, advantage, partner):
    rows = queries.shape[0]

    def by_head(array):
        return array.reshape(array.shape[0], KV_HEADS, -1).transpose(1, 0, 2)

    def swap(array):
        return lax.all_to_all(array, "head", split_axis=0, concat_axis=0, tiled=True)

    x, z, core = (lax.axis_index(name) for name in TREES)
    head = lax.axis_index("head")
    member = jnp.arange(X * CORE)
    to_x = partner[((x + member // CORE) % X * Z + z) * CORE + member % CORE] // CORE % Z
    cores = jnp.stack([core, 1 - core])
    mates = partner[(x * Z + z) * CORE + cores]
    to_core = jnp.concatenate([(x - mates // (Z * CORE)) % X, cores]).astype(jnp.int32)
    crossed = mates[0] % CORE != core
    ints = jnp.concatenate([lengths[0], guests[0], crossed[None]]).astype(jnp.int32)

    prompt = swap(jnp.concatenate([by_head(keys[:PROMPT]), by_head(values[:PROMPT])], axis=2))[0]
    qkv = swap(jnp.concatenate([by_head(queries), by_head(keys), by_head(values)], axis=2))
    far = exchange(prompt, to_x, to_core)
    grads, far_grad, own = attention(
        ints, advantage[0], qkv.reshape(ROWS, -1), prompt, upstream, *far
    )
    grads = swap(grads.reshape(KV_HEADS, rows, -1))
    stay, cross = exchange(far_grad, to_x, to_core)
    first = (own + jnp.where(crossed, cross, stay).astype(jnp.float32)).astype(jnp.bfloat16)
    first, grads = lax.optimization_barrier((first, grads))
    first = swap(jnp.broadcast_to(first[None], (KV_HEADS, PROMPT, KV)))

    def by_row(array):
        return array.transpose(1, 0, 2).reshape(array.shape[1], -1)

    def finish(lanes):
        main = by_row(grads[:, :, Q:][:, :, lanes])
        top = jnp.where(head == 0, by_row(first[:, :, lanes]), main[:PROMPT])
        return jnp.concatenate([top, main[PROMPT:]], axis=0)

    return (
        by_row(grads[:, :, :Q]),
        finish(slice(0, HEAD_DIM)),
        finish(slice(HEAD_DIM, KV)),
    )


def solution(mesh):
    mesh = Mesh(mesh.devices.reshape(X, Z, CORE, KV_HEADS), TREES + ("head",))
    tokens = P(TREES + ("head",), None)
    trees = P(TREES, None)
    return jax.shard_map(
        local,
        mesh=mesh,
        in_specs=(tokens, tokens, tokens, P(TREES, "head"), trees, trees, trees, P()),
        out_specs=(tokens, tokens, tokens),
        check_vma=False,
    )
```

```python
import jax
import jax.numpy as jnp
from jax import lax
from jax.experimental import pallas as pl
from jax.experimental.pallas import tpu as pltpu
from jax.sharding import Mesh, PartitionSpec as P

HEAD_DIM = 128
PROMPT = 48
RESP = 8
RESP_LEN = 122
ROWS = 1024
GROUP = 4
KV_HEADS = 8
WINDOW = 128
Q = GROUP * HEAD_DIM
KV = 2 * HEAD_DIM
TREES = ("x", "z", "core")
PLANE = ("x", "core")
X, Z, CORE = 4, 12, 2


def attend(q_rows, keys, vals, cot, allowed):
    scaling = HEAD_DIM ** (-0.5)
    nt = (((1,), (1,)), ((), ()))
    scores = lax.dot_general(keys, q_rows, nt, preferred_element_type=jnp.float32) * scaling
    scores = jnp.where(allowed, scores, -jnp.inf)
    lifted = jnp.exp(scores - jnp.max(scores, axis=0, keepdims=True))
    probs = lifted * (1.0 / jnp.sum(lifted, axis=0, keepdims=True))
    probs_low = probs.astype(jnp.bfloat16)
    grad_probs = lax.dot_general(vals, cot, nt, preferred_element_type=jnp.float32)
    inner = jnp.sum(probs_low.astype(jnp.float32) * grad_probs, axis=0, keepdims=True)
    grad_scores = (probs * (grad_probs - inner) * scaling).astype(jnp.bfloat16)
    grad_v = jnp.dot(probs_low, cot, preferred_element_type=jnp.float32)
    grad_k = jnp.dot(grad_scores, q_rows, preferred_element_type=jnp.float32)
    tn = (((0,), (0,)), ((), ()))
    grad_q = lax.dot_general(grad_scores, keys, tn, preferred_element_type=jnp.float32)
    return grad_q, jnp.concatenate([grad_k, grad_v], axis=1)


def stack_heads(block):
    return jnp.concatenate(
        [block[:, j * HEAD_DIM : (j + 1) * HEAD_DIM] for j in range(GROUP)], axis=0
    )


def unstack_heads(block, rows):
    return jnp.concatenate([block[j * rows : (j + 1) * rows] for j in range(GROUP)], axis=1)


def attention_kernel(
    partner, lengths, guests, adv, qkv, cot_ref, far_in, grads, far_out, own_out, pre, acc
):
    iota = lax.broadcasted_iota
    pre[0] = qkv[:PROMPT, Q:]
    pre[1] = far_in[partner_entry(partner)]
    acc[1] = jnp.zeros((PROMPT, KV), jnp.float32)

    wide = (PROMPT, GROUP * PROMPT)
    query = iota(jnp.int32, wide, 1)
    for j in range(1, GROUP):
        query = jnp.where(query >= PROMPT, query - PROMPT, query)
    grad_q, grad_kv = attend(
        stack_heads(qkv[:PROMPT, :Q]),
        pre[0, :, :HEAD_DIM],
        pre[0, :, HEAD_DIM:],
        stack_heads(cot_ref[:PROMPT, :]),
        iota(jnp.int32, wide, 0) <= query,
    )
    grads[:PROMPT, :Q] = unstack_heads(grad_q, PROMPT).astype(jnp.bfloat16)
    grads[:PROMPT, Q:] = jnp.zeros((PROMPT, KV), jnp.bfloat16)
    acc[0] = grad_kv

    for slot in range(RESP):
        first = PROMPT + RESP_LEN * slot
        start = first // 8 * 8
        skip = first - start
        rows = slice(start, start + WINDOW)
        guest = guests[0, slot]
        keys = jnp.concatenate([pre[guest, :, :HEAD_DIM], qkv[rows, Q : Q + HEAD_DIM]], axis=0)
        vals = jnp.concatenate([pre[guest, :, HEAD_DIM:], qkv[rows, Q + HEAD_DIM :]], axis=0)
        token = iota(jnp.int32, (WINDOW, Q), 0) - skip
        weight = jnp.where((token >= 0) & (token < lengths[0, slot]), adv[0, slot], 0.0)
        cot = (cot_ref[rows, :].astype(jnp.float32) * weight).astype(jnp.bfloat16)
        shape = (PROMPT + WINDOW, GROUP * WINDOW)
        key = iota(jnp.int32, shape, 0)
        query = iota(jnp.int32, shape, 1) & (WINDOW - 1)
        allowed = (key < PROMPT) | ((key >= PROMPT + skip) & (key - PROMPT <= query))
        grad_q, grad_kv = attend(stack_heads(qkv[rows, :Q]), keys, vals, stack_heads(cot), allowed)
        acc[guest] += grad_kv[:PROMPT]
        new = jnp.concatenate([unstack_heads(grad_q, WINDOW), grad_kv[PROMPT:]], axis=1)
        if skip:
            old = grads[start : start + 8, :].astype(jnp.float32)
            top = jnp.where(iota(jnp.int32, old.shape, 0) < skip, old, new[:8])
            new = jnp.concatenate([top, new[8:]], axis=0)
        grads[rows, :] = new.astype(jnp.bfloat16)

    own_out[...] = acc[0]
    far_out[...] = acc[1].astype(jnp.bfloat16)


VMEM = pl.BlockSpec(memory_space=pltpu.VMEM)
SMEM = pl.BlockSpec(memory_space=pltpu.SMEM)
SMALL = pltpu.CompilerParams(vmem_limit_bytes=8 * 2**20)
LARGE = pltpu.CompilerParams(vmem_limit_bytes=24 * 2**20)


def attention(partner, lengths, guests, adv, qkv, cot, far):
    return pl.pallas_call(
        attention_kernel,
        out_shape=(
            jax.ShapeDtypeStruct((ROWS, Q + KV), jnp.bfloat16),
            jax.ShapeDtypeStruct((PROMPT, KV), jnp.bfloat16),
            jax.ShapeDtypeStruct((PROMPT, KV), jnp.float32),
        ),
        in_specs=[SMEM] * 4 + [VMEM] * 3,
        out_specs=(VMEM, VMEM, VMEM),
        scratch_shapes=[
            pltpu.VMEM((2, PROMPT, KV), jnp.bfloat16),
            pltpu.VMEM((2, PROMPT, KV), jnp.float32),
        ],
        cost_estimate=pl.CostEstimate(flops=10**9, transcendentals=720896, bytes_accessed=5 * 2**20),
        compiler_params=LARGE,
        name="attention",
    )(partner, lengths, guests, adv, qkv, cot, far)


def place():
    return tuple(lax.axis_index(name) for name in TREES)


def pick_kernel(partner, blocks, out):
    _, z, core = place()
    for i in range(X):
        wanted = partner[(i * Z + z) * CORE + core]
        out[i] = blocks[lax.rem(wanted, Z * CORE)]


def pick(partner, blocks):
    return pl.pallas_call(
        pick_kernel,
        out_shape=jax.ShapeDtypeStruct((X,) + blocks.shape[1:], blocks.dtype),
        in_specs=[SMEM, VMEM],
        out_specs=VMEM,
        cost_estimate=pl.CostEstimate(flops=0, transcendentals=0, bytes_accessed=2**18),
        compiler_params=SMALL,
        name="pick",
    )(partner, blocks)


def exchange(block, partner):
    wanted = pick(partner, lax.all_gather(block, ("z", "core")))
    return lax.all_gather(wanted, "x", axis=0, tiled=True)


def partner_entry(partner):
    x, z, core = place()
    return X * lax.div(partner[(x * Z + z) * CORE + core], Z * CORE) + x


def lay_out_kernel(keys, values, out):
    for i in range(KV_HEADS):
        lanes = slice(i * HEAD_DIM, (i + 1) * HEAD_DIM)
        out[i, :, :HEAD_DIM] = keys[:, lanes]
        out[i, :, HEAD_DIM:] = values[:, lanes]


def lay_out(keys, values):
    rows = pl.BlockSpec((PROMPT, KV_HEADS * HEAD_DIM), lambda i: (0, 0))
    return pl.pallas_call(
        lay_out_kernel,
        grid=(1,),
        out_shape=jax.ShapeDtypeStruct((KV_HEADS, PROMPT, KV), jnp.bfloat16),
        in_specs=[rows, rows],
        out_specs=pl.BlockSpec((KV_HEADS, PROMPT, KV), lambda i: (0, 0, 0)),
        cost_estimate=pl.CostEstimate(flops=0, transcendentals=0, bytes_accessed=2**19),
        compiler_params=SMALL,
        name="lay_out",
    )(keys, values)


def by_token_kernel(main, first, grad_k, grad_v):
    owner = lax.axis_index("head") == 0
    for i in range(KV_HEADS):
        lanes = slice(i * HEAD_DIM, (i + 1) * HEAD_DIM)
        for ref, start in ((grad_k, 0), (grad_v, HEAD_DIM)):
            part = slice(start, start + HEAD_DIM)
            old = main[i, :PROMPT, part].astype(jnp.float32)
            top = jnp.where(owner, first[i, :, part].astype(jnp.float32), old)
            ref[:PROMPT, lanes] = top.astype(ref.dtype)
            ref[PROMPT:, lanes] = main[i, PROMPT:, part]


def by_token(grads, first):
    rows = grads.shape[1]
    out = jax.ShapeDtypeStruct((rows, KV_HEADS * HEAD_DIM), jnp.bfloat16)
    whole = pl.BlockSpec(out.shape, lambda i: (0, 0))
    return pl.pallas_call(
        by_token_kernel,
        grid=(1,),
        out_shape=(out, out),
        in_specs=[
            pl.BlockSpec((KV_HEADS, rows, KV), lambda i: (0, 0, Q // KV)),
            pl.BlockSpec((KV_HEADS, PROMPT, KV), lambda i: (0, 0, 0)),
        ],
        out_specs=(whole, whole),
        cost_estimate=pl.CostEstimate(flops=0, transcendentals=0, bytes_accessed=2**20),
        compiler_params=SMALL,
        name="by_token",
    )(grads, first)


def finish_kernel(partner, own, back, out):
    block = own[...] + back[partner_entry(partner)].astype(jnp.float32)
    for i in range(KV_HEADS):
        out[i] = block.astype(out.dtype)


def finish(partner, own, back):
    return pl.pallas_call(
        finish_kernel,
        out_shape=jax.ShapeDtypeStruct((KV_HEADS,) + own.shape, jnp.bfloat16),
        in_specs=[SMEM, VMEM, VMEM],
        out_specs=VMEM,
        cost_estimate=pl.CostEstimate(flops=0, transcendentals=0, bytes_accessed=2**18),
        compiler_params=SMALL,
        name="finish",
    )(partner, own, back)


def local(queries, keys, values, upstream, lengths, guests, advantage, partner):
    rows = queries.shape[0]

    def by_head(array):
        return array.reshape(array.shape[0], KV_HEADS, -1).transpose(1, 0, 2)

    def swap(array):
        return lax.all_to_all(array, "head", split_axis=0, concat_axis=0, tiled=True)

    prompt = swap(lay_out(keys, values))
    qkv = swap(jnp.concatenate([by_head(queries), by_head(keys), by_head(values)], axis=2))
    far = exchange(prompt[0], partner)
    grads, far_grad, own = attention(
        partner, lengths, guests, advantage, qkv.reshape(ROWS, -1), upstream, far
    )
    grads = swap(grads.reshape(KV_HEADS, rows, -1))
    first = finish(partner, own, exchange(far_grad, partner))
    first, grads = lax.optimization_barrier((first, grads))
    first = swap(first)
    grad_q = grads[:, :, :Q].transpose(1, 0, 2).reshape(rows, -1)
    return (grad_q,) + tuple(by_token(grads, first))


def solution(mesh):
    mesh = Mesh(mesh.devices.reshape(X, Z, CORE, KV_HEADS), TREES + ("head",))
    tokens = P(TREES + ("head",), None)
    trees = P(TREES, None)
    return jax.shard_map(
        local,
        mesh=mesh,
        in_specs=(tokens, tokens, tokens, P(TREES, "head"), trees, trees, trees, P()),
        out_specs=(tokens, tokens, tokens),
        check_vma=False,
    )
```

```python
import jax
import jax.numpy as jnp
from jax import lax
from jax.experimental import pallas as pl
from jax.experimental.pallas import tpu as pltpu
from jax.sharding import Mesh, PartitionSpec as P

HEAD_DIM = 128
PROMPT = 48
RESP = 8
RESP_LEN = 122
ROWS = 1024
GROUP = 4
KV_HEADS = 8
WINDOW = 128
Q = GROUP * HEAD_DIM
KV = 2 * HEAD_DIM
TREES = ("x", "z", "core")
PLANE = ("x", "core")
X, Z, CORE = 4, 12, 2


NT = (((1,), (1,)), ((), ()))
TN = (((0,), (0,)), ((), ()))
SCALING = HEAD_DIM ** (-0.5)
LOG2_E = 1.4426950408889634


def products(q_rows, keys, vals, cot):
    scores = lax.dot_general(keys, q_rows, NT, preferred_element_type=jnp.float32)
    grad_probs = lax.dot_general(vals, cot, NT, preferred_element_type=jnp.float32)
    return scores * (SCALING * LOG2_E), grad_probs


def backward(scores, grad_probs, q_rows, keys, cot):
    lifted = jnp.exp2(scores - jnp.max(scores, axis=0, keepdims=True))
    share = 1.0 / jnp.sum(lifted, axis=0, keepdims=True)
    inner = jnp.sum(lifted * grad_probs, axis=0, keepdims=True) * share
    probs = lifted * share
    grad_scores = (probs * (grad_probs - inner) * SCALING).astype(jnp.bfloat16)
    grad_v = jnp.dot(probs.astype(jnp.bfloat16), cot, preferred_element_type=jnp.float32)
    grad_k = jnp.dot(grad_scores, q_rows, preferred_element_type=jnp.float32)
    grad_q = lax.dot_general(grad_scores, keys, TN, preferred_element_type=jnp.float32)
    return grad_q, jnp.concatenate([grad_k, grad_v], axis=1)


def stack_heads(block):
    return jnp.concatenate(
        [block[:, j * HEAD_DIM : (j + 1) * HEAD_DIM] for j in range(GROUP)], axis=0
    )


def unstack_heads(block, rows):
    return jnp.concatenate([block[j * rows : (j + 1) * rows] for j in range(GROUP)], axis=1)


def attention_kernel(
    partner, lengths, guests, adv, qkv, cot_ref, far_in, grads, far_out, own_out, pre, acc, later
):
    iota = lax.broadcasted_iota
    pre[0] = qkv[:PROMPT, Q:]
    pre[1] = far_in[partner_entry(partner)]
    acc[1] = jnp.zeros((PROMPT, KV), jnp.float32)
    causal = iota(jnp.int32, later.shape, 0) <= iota(jnp.int32, later.shape, 1)
    later[...] = jnp.where(causal, 0.0, -jnp.inf)

    def window(slot):
        first = PROMPT + RESP_LEN * slot
        start = first // 8 * 8
        return slice(start, start + WINDOW), first - start

    def load(slot):
        rows, skip = window(slot)
        guest = guests[0, slot]
        q_rows = stack_heads(qkv[rows, :Q])
        keys = jnp.concatenate([pre[guest, :, :HEAD_DIM], qkv[rows, Q : Q + HEAD_DIM]], axis=0)
        vals = jnp.concatenate([pre[guest, :, HEAD_DIM:], qkv[rows, Q + HEAD_DIM :]], axis=0)
        token = iota(jnp.int32, (WINDOW, HEAD_DIM), 0) - skip
        weight = jnp.where((token >= 0) & (token < lengths[0, slot]), adv[0, slot], 0.0)
        cot = jnp.concatenate(
            [
                (cot_ref[rows, lanes].astype(jnp.float32) * weight).astype(jnp.bfloat16)
                for lanes in (slice(j * HEAD_DIM, (j + 1) * HEAD_DIM) for j in range(GROUP))
            ],
            axis=0,
        )
        return (q_rows, keys, cot), products(q_rows, keys, vals, cot)

    def emit(slot, operands, scores, grad_probs):
        rows, skip = window(slot)
        bias = later[...]
        if skip:
            top = jnp.where(iota(jnp.int32, (8, WINDOW), 0) < skip, -jnp.inf, bias[:8])
            bias = jnp.concatenate([top, bias[8:]], axis=0)
        bias = jnp.concatenate([bias] * GROUP, axis=1)
        scores = jnp.concatenate([scores[:PROMPT], scores[PROMPT:] + bias], axis=0)
        grad_q, grad_kv = backward(scores, grad_probs, *operands)
        acc[guests[0, slot]] += grad_kv[:PROMPT]
        new = jnp.concatenate([unstack_heads(grad_q, WINDOW), grad_kv[PROMPT:]], axis=1)
        if skip:
            old = grads[rows.start : rows.start + 8, :].astype(jnp.float32)
            top = jnp.where(iota(jnp.int32, old.shape, 0) < skip, old, new[:8])
            new = jnp.concatenate([top, new[8:]], axis=0)
        grads[rows, :] = new.astype(jnp.bfloat16)

    q_rows = stack_heads(qkv[:PROMPT, :Q])
    cot = stack_heads(cot_ref[:PROMPT, :])
    keys = pre[0, :, :HEAD_DIM]
    scores, grad_probs = products(q_rows, keys, pre[0, :, HEAD_DIM:], cot)
    query = iota(jnp.int32, scores.shape, 1)
    for j in range(1, GROUP):
        query = jnp.where(query >= PROMPT, query - PROMPT, query)
    scores = jnp.where(iota(jnp.int32, scores.shape, 0) <= query, scores, -jnp.inf)
    grad_q, acc[0] = backward(scores, grad_probs, q_rows, keys, cot)
    grads[:PROMPT, :Q] = unstack_heads(grad_q, PROMPT).astype(jnp.bfloat16)
    grads[:PROMPT, Q:] = jnp.zeros((PROMPT, KV), jnp.bfloat16)

    ahead = load(0)
    for slot in range(RESP):
        operands, parts = ahead
        if slot + 1 < RESP:
            ahead = load(slot + 1)
        emit(slot, operands, *parts)
    own_out[...] = acc[0]
    far_out[...] = acc[1].astype(jnp.bfloat16)


VMEM = pl.BlockSpec(memory_space=pltpu.VMEM)
SMEM = pl.BlockSpec(memory_space=pltpu.SMEM)
SMALL = pltpu.CompilerParams(vmem_limit_bytes=8 * 2**20)
LARGE = pltpu.CompilerParams(vmem_limit_bytes=24 * 2**20)


def attention(partner, lengths, guests, adv, qkv, cot, far):
    return pl.pallas_call(
        attention_kernel,
        out_shape=(
            jax.ShapeDtypeStruct((ROWS, Q + KV), jnp.bfloat16),
            jax.ShapeDtypeStruct((PROMPT, KV), jnp.bfloat16),
            jax.ShapeDtypeStruct((PROMPT, KV), jnp.float32),
        ),
        in_specs=[SMEM] * 4 + [VMEM] * 3,
        out_specs=(VMEM, VMEM, VMEM),
        scratch_shapes=[
            pltpu.VMEM((2, PROMPT, KV), jnp.bfloat16),
            pltpu.VMEM((2, PROMPT, KV), jnp.float32),
            pltpu.VMEM((WINDOW, WINDOW), jnp.float32),
        ],
        cost_estimate=pl.CostEstimate(flops=10**9, transcendentals=720896, bytes_accessed=5 * 2**20),
        compiler_params=LARGE,
        name="attention",
    )(partner, lengths, guests, adv, qkv, cot, far)


def place():
    return tuple(lax.axis_index(name) for name in TREES)


def pick_kernel(partner, blocks, out):
    _, z, core = place()
    for i in range(X):
        wanted = partner[(i * Z + z) * CORE + core]
        out[i] = blocks[lax.rem(wanted, Z * CORE)]


def pick(partner, blocks):
    return pl.pallas_call(
        pick_kernel,
        out_shape=jax.ShapeDtypeStruct((X,) + blocks.shape[1:], blocks.dtype),
        in_specs=[SMEM, VMEM],
        out_specs=VMEM,
        cost_estimate=pl.CostEstimate(flops=0, transcendentals=0, bytes_accessed=2**18),
        compiler_params=SMALL,
        name="pick",
    )(partner, blocks)


def exchange(block, partner):
    wanted = pick(partner, lax.all_gather(block, ("z", "core")))
    return lax.all_gather(wanted, "x", axis=0, tiled=True)


def partner_entry(partner):
    x, z, core = place()
    return X * lax.div(partner[(x * Z + z) * CORE + core], Z * CORE) + x


def lay_out_kernel(keys, values, out):
    for i in range(KV_HEADS):
        lanes = slice(i * HEAD_DIM, (i + 1) * HEAD_DIM)
        out[i, :, :HEAD_DIM] = keys[:, lanes]
        out[i, :, HEAD_DIM:] = values[:, lanes]


def lay_out(keys, values):
    rows = pl.BlockSpec((PROMPT, KV_HEADS * HEAD_DIM), lambda i: (0, 0))
    return pl.pallas_call(
        lay_out_kernel,
        grid=(1,),
        out_shape=jax.ShapeDtypeStruct((KV_HEADS, PROMPT, KV), jnp.bfloat16),
        in_specs=[rows, rows],
        out_specs=pl.BlockSpec((KV_HEADS, PROMPT, KV), lambda i: (0, 0, 0)),
        cost_estimate=pl.CostEstimate(flops=0, transcendentals=0, bytes_accessed=2**19),
        name="lay_out",
    )(keys, values)


def by_token_kernel(main, first, grad_k, grad_v):
    owner = lax.axis_index("head") == 0
    for i in range(KV_HEADS):
        lanes = slice(i * HEAD_DIM, (i + 1) * HEAD_DIM)
        for ref, start in ((grad_k, 0), (grad_v, HEAD_DIM)):
            part = slice(start, start + HEAD_DIM)
            old = main[i, :PROMPT, part].astype(jnp.float32)
            top = jnp.where(owner, first[i, :, part].astype(jnp.float32), old)
            ref[:PROMPT, lanes] = top.astype(ref.dtype)
            ref[PROMPT:, lanes] = main[i, PROMPT:, part]


def by_token(grads, first):
    rows = grads.shape[1]
    out = jax.ShapeDtypeStruct((rows, KV_HEADS * HEAD_DIM), jnp.bfloat16)
    whole = pl.BlockSpec(out.shape, lambda i: (0, 0))
    return pl.pallas_call(
        by_token_kernel,
        grid=(1,),
        out_shape=(out, out),
        in_specs=[
            pl.BlockSpec((KV_HEADS, rows, KV), lambda i: (0, 0, Q // KV)),
            pl.BlockSpec((KV_HEADS, PROMPT, KV), lambda i: (0, 0, 0)),
        ],
        out_specs=(whole, whole),
        cost_estimate=pl.CostEstimate(flops=0, transcendentals=0, bytes_accessed=2**20),
        compiler_params=SMALL,
        name="by_token",
    )(grads, first)


def finish_kernel(partner, own, back, out):
    block = own[...] + back[partner_entry(partner)].astype(jnp.float32)
    for i in range(KV_HEADS):
        out[i] = block.astype(out.dtype)


def finish(partner, own, back):
    return pl.pallas_call(
        finish_kernel,
        out_shape=jax.ShapeDtypeStruct((KV_HEADS,) + own.shape, jnp.bfloat16),
        in_specs=[SMEM, VMEM, VMEM],
        out_specs=VMEM,
        cost_estimate=pl.CostEstimate(flops=0, transcendentals=0, bytes_accessed=2**18),
        compiler_params=SMALL,
        name="finish",
    )(partner, own, back)


def local(queries, keys, values, upstream, lengths, guests, advantage, partner):
    rows = queries.shape[0]

    def by_head(array):
        return array.reshape(array.shape[0], KV_HEADS, -1).transpose(1, 0, 2)

    def swap(array):
        return lax.all_to_all(array, "head", split_axis=0, concat_axis=0, tiled=True)

    prompt = swap(lay_out(keys, values))
    qkv = swap(jnp.concatenate([by_head(queries), by_head(keys), by_head(values)], axis=2))
    far = exchange(prompt[0], partner)
    grads, far_grad, own = attention(
        partner, lengths, guests, advantage, qkv.reshape(ROWS, -1), upstream, far
    )
    grads = swap(grads.reshape(KV_HEADS, rows, -1))
    first = finish(partner, own, exchange(far_grad, partner))
    first, grads = lax.optimization_barrier((first, grads))
    first = swap(first)
    grad_q = grads[:, :, :Q].transpose(1, 0, 2).reshape(rows, -1)
    return (grad_q,) + tuple(by_token(grads, first))


def solution(mesh):
    mesh = Mesh(mesh.devices.reshape(X, Z, CORE, KV_HEADS), TREES + ("head",))
    tokens = P(TREES + ("head",), None)
    trees = P(TREES, None)
    return jax.shard_map(
        local,
        mesh=mesh,
        in_specs=(tokens, tokens, tokens, P(TREES, "head"), trees, trees, trees, P()),
        out_specs=(tokens, tokens, tokens),
        check_vma=False,
    )
```

```python
import jax
import jax.numpy as jnp
from jax import lax
from jax.experimental import pallas as pl
from jax.experimental.pallas import tpu as pltpu
from jax.sharding import Mesh, PartitionSpec as P

HEAD_DIM = 128
PROMPT = 48
RESP = 8
RESP_LEN = 122
ROWS = 1024
GROUP = 4
KV_HEADS = 8
WINDOW = 128
Q = GROUP * HEAD_DIM
KV = 2 * HEAD_DIM
BLOCK = ROWS // KV_HEADS
REST = BLOCK - PROMPT
PACKED = REST + 2 * BLOCK
TREES = ("x", "z", "core")
PLANE = ("x", "core")
X, Z, CORE = 4, 12, 2


NT = (((1,), (1,)), ((), ()))
TN = (((0,), (0,)), ((), ()))
SCALING = HEAD_DIM ** (-0.5)
LOG2_E = 1.4426950408889634


def products(q_rows, keys, vals, cot):
    scores = lax.dot_general(keys, q_rows, NT, preferred_element_type=jnp.float32)
    grad_probs = lax.dot_general(vals, cot, NT, preferred_element_type=jnp.float32)
    return scores * (SCALING * LOG2_E), grad_probs


def backward(scores, grad_probs, q_rows, keys, cot):
    lifted = jnp.exp2(scores - jnp.max(scores, axis=0, keepdims=True))
    share = 1.0 / jnp.sum(lifted, axis=0, keepdims=True)
    inner = jnp.sum(lifted * grad_probs, axis=0, keepdims=True) * share
    probs = lifted * share
    grad_scores = (probs * (grad_probs - inner) * SCALING).astype(jnp.bfloat16)
    grad_v = jnp.dot(probs.astype(jnp.bfloat16), cot, preferred_element_type=jnp.float32)
    grad_k = jnp.dot(grad_scores, q_rows, preferred_element_type=jnp.float32)
    grad_q = lax.dot_general(grad_scores, keys, TN, preferred_element_type=jnp.float32)
    return grad_q, jnp.concatenate([grad_k, grad_v], axis=1)


def stack_heads(block):
    return jnp.concatenate(
        [block[:, j * HEAD_DIM : (j + 1) * HEAD_DIM] for j in range(GROUP)], axis=0
    )


def segments(start, rows):
    found, at = [], start
    while at < start + rows:
        block, first = divmod(at, BLOCK)
        last = min(PROMPT if first < PROMPT else BLOCK, first + start + rows - at)
        found.append((block, first, last, at - start))
        at += last - first
    return found


def q_index(block, first, last, head):
    shift = REST + head // 2 * BLOCK
    lanes = slice(head % 2 * HEAD_DIM, (head % 2 + 1) * HEAD_DIM)
    return block, slice(shift + first, shift + last), lanes


def kv_index(packed, low, block, first, last):
    if first < PROMPT:
        return low, (block, slice(first, last))
    return packed, (block, slice(first - PROMPT, last - PROMPT))


def attention_kernel(
    partner, lengths, guests, adv, packed, low, cot_ref, far_in, grads, grads_low, far_out, own_out, pre, acc, later
):
    iota = lax.broadcasted_iota
    pre[0] = low[0]
    pre[1] = far_in[partner_entry(partner)]
    acc[1] = jnp.zeros((PROMPT, KV), jnp.float32)
    causal = iota(jnp.int32, later.shape, 0) <= iota(jnp.int32, later.shape, 1)
    later[...] = jnp.where(causal, 0.0, -jnp.inf)

    def q_of(start, rows):
        return jnp.concatenate(
            [
                packed[q_index(block, first, last, head)]
                for head in range(GROUP)
                for block, first, last, _ in segments(start, rows)
            ],
            axis=0,
        )

    def kv_of(start, rows):
        parts = []
        for block, first, last, _ in segments(start, rows):
            ref, index = kv_index(packed, low, block, first, last)
            parts.append(ref[index])
        return parts

    def window(slot):
        first = PROMPT + RESP_LEN * slot
        start = first // 8 * 8
        return slice(start, start + WINDOW), first - start

    def load(slot):
        rows, skip = window(slot)
        guest = guests[0, slot]
        q_rows = q_of(rows.start, WINDOW)
        kv = jnp.concatenate([pre[guest]] + kv_of(rows.start, WINDOW), axis=0)
        keys, vals = kv[:, :HEAD_DIM], kv[:, HEAD_DIM:]
        token = iota(jnp.int32, (WINDOW, HEAD_DIM), 0) - skip
        weight = jnp.where((token >= 0) & (token < lengths[0, slot]), adv[0, slot], 0.0)
        cot = jnp.concatenate(
            [
                (cot_ref[rows, lanes].astype(jnp.float32) * weight).astype(jnp.bfloat16)
                for lanes in (slice(j * HEAD_DIM, (j + 1) * HEAD_DIM) for j in range(GROUP))
            ],
            axis=0,
        )
        return (q_rows, keys, cot), products(q_rows, keys, vals, cot)

    def emit(slot, operands, scores, grad_probs):
        rows, skip = window(slot)
        bias = later[...]
        if skip:
            top = jnp.where(iota(jnp.int32, (8, WINDOW), 0) < skip, -jnp.inf, bias[:8])
            bias = jnp.concatenate([top, bias[8:]], axis=0)
        bias = jnp.concatenate([bias] * GROUP, axis=1)
        scores = jnp.concatenate([scores[:PROMPT], scores[PROMPT:] + bias], axis=0)
        grad_q, grad_kv = backward(scores, grad_probs, *operands)
        acc[guests[0, slot]] += grad_kv[:PROMPT]
        for block, first, last, at in segments(rows.start, WINDOW):
            for head in range(GROUP):
                new = grad_q[head * WINDOW + at : head * WINDOW + at + last - first]
                store(grads, q_index(block, first, last, head), new, skip if at == 0 else 0)
            ref, index = kv_index(grads, grads_low, block, first, last)
            new = grad_kv[PROMPT + at : PROMPT + at + last - first]
            store(ref, index, new, skip if at == 0 else 0)

    def store(ref, index, new, skip):
        if skip:
            block, rows, *lanes = index
            old = ref[(block, slice(rows.start, rows.start + 8), *lanes)].astype(jnp.float32)
            top = jnp.where(iota(jnp.int32, old.shape, 0) < skip, old, new[:8])
            new = jnp.concatenate([top, new[8:]], axis=0) if new.shape[0] > 8 else top
        ref[index] = new.astype(jnp.bfloat16)

    q_rows = q_of(0, PROMPT)
    cot = stack_heads(cot_ref[:PROMPT, :])
    keys = pre[0, :, :HEAD_DIM]
    scores, grad_probs = products(q_rows, keys, pre[0, :, HEAD_DIM:], cot)
    query = iota(jnp.int32, scores.shape, 1)
    for j in range(1, GROUP):
        query = jnp.where(query >= PROMPT, query - PROMPT, query)
    scores = jnp.where(iota(jnp.int32, scores.shape, 0) <= query, scores, -jnp.inf)
    grad_q, acc[0] = backward(scores, grad_probs, q_rows, keys, cot)
    for head in range(GROUP):
        new = grad_q[head * PROMPT : (head + 1) * PROMPT]
        store(grads, q_index(0, 0, PROMPT, head), new, 0)

    ahead = load(0)
    for slot in range(RESP):
        operands, parts = ahead
        if slot + 1 < RESP:
            ahead = load(slot + 1)
        emit(slot, operands, *parts)
    own_out[...] = acc[0]
    grads_low[0] = acc[0].astype(jnp.bfloat16)
    far_out[...] = acc[1].astype(jnp.bfloat16)


VMEM = pl.BlockSpec(memory_space=pltpu.VMEM)
SMEM = pl.BlockSpec(memory_space=pltpu.SMEM)
SMALL = pltpu.CompilerParams(vmem_limit_bytes=8 * 2**20)
LARGE = pltpu.CompilerParams(vmem_limit_bytes=24 * 2**20)


def attention(partner, lengths, guests, adv, packed, low, cot, far):
    return pl.pallas_call(
        attention_kernel,
        out_shape=(
            jax.ShapeDtypeStruct(packed.shape, jnp.bfloat16),
            jax.ShapeDtypeStruct(low.shape, jnp.bfloat16),
            jax.ShapeDtypeStruct((PROMPT, KV), jnp.bfloat16),
            jax.ShapeDtypeStruct((PROMPT, KV), jnp.float32),
        ),
        in_specs=[SMEM] * 4 + [VMEM] * 4,
        out_specs=(VMEM,) * 4,
        scratch_shapes=[
            pltpu.VMEM((2, PROMPT, KV), jnp.bfloat16),
            pltpu.VMEM((2, PROMPT, KV), jnp.float32),
            pltpu.VMEM((WINDOW, WINDOW), jnp.float32),
        ],
        cost_estimate=pl.CostEstimate(flops=10**9, transcendentals=720896, bytes_accessed=5 * 2**20),
        compiler_params=LARGE,
        name="attention",
    )(partner, lengths, guests, adv, packed, low, cot, far)


def place():
    return tuple(lax.axis_index(name) for name in TREES)


def pick_kernel(partner, blocks, out):
    _, z, core = place()
    for i in range(X):
        wanted = partner[(i * Z + z) * CORE + core]
        out[i] = blocks[lax.rem(wanted, Z * CORE)]


def pick(partner, blocks):
    return pl.pallas_call(
        pick_kernel,
        out_shape=jax.ShapeDtypeStruct((X,) + blocks.shape[1:], blocks.dtype),
        in_specs=[SMEM, VMEM],
        out_specs=VMEM,
        cost_estimate=pl.CostEstimate(flops=0, transcendentals=0, bytes_accessed=2**18),
        compiler_params=SMALL,
        name="pick",
    )(partner, blocks)


def exchange(block, partner):
    wanted = pick(partner, lax.all_gather(block, ("z", "core")))
    return lax.all_gather(wanted, "x", axis=0, tiled=True)


def partner_entry(partner):
    x, z, core = place()
    return X * lax.div(partner[(x * Z + z) * CORE + core], Z * CORE) + x


def lay_out_kernel(keys, values, out):
    for i in range(KV_HEADS):
        lanes = slice(i * HEAD_DIM, (i + 1) * HEAD_DIM)
        out[i, :, :HEAD_DIM] = keys[:, lanes]
        out[i, :, HEAD_DIM:] = values[:, lanes]


def lay_out(keys, values):
    rows = pl.BlockSpec((PROMPT, KV_HEADS * HEAD_DIM), lambda i: (0, 0))
    return pl.pallas_call(
        lay_out_kernel,
        grid=(1,),
        out_shape=jax.ShapeDtypeStruct((KV_HEADS, PROMPT, KV), jnp.bfloat16),
        in_specs=[rows, rows],
        out_specs=pl.BlockSpec((KV_HEADS, PROMPT, KV), lambda i: (0, 0, 0)),
        cost_estimate=pl.CostEstimate(flops=0, transcendentals=0, bytes_accessed=2**19),
        name="lay_out",
    )(keys, values)


def pack_kernel(queries, keys, values, out):
    for i in range(KV_HEADS):
        lanes = slice(i * HEAD_DIM, (i + 1) * HEAD_DIM)
        out[i, :REST, :HEAD_DIM] = keys[PROMPT:, lanes]
        out[i, :REST, HEAD_DIM:] = values[PROMPT:, lanes]
        out[i, REST : REST + BLOCK] = queries[:, i * Q : i * Q + KV]
        out[i, REST + BLOCK :] = queries[:, i * Q + KV : (i + 1) * Q]


def pack(queries, keys, values):
    return pl.pallas_call(
        pack_kernel,
        out_shape=jax.ShapeDtypeStruct((KV_HEADS, PACKED, KV), jnp.bfloat16),
        in_specs=[VMEM] * 3,
        out_specs=VMEM,
        cost_estimate=pl.CostEstimate(flops=0, transcendentals=0, bytes_accessed=3 * 2**20),
        compiler_params=SMALL,
        name="pack",
    )(queries, keys, values)


def q_by_token_kernel(grads, out):
    for i in range(KV_HEADS):
        out[:, i * Q : i * Q + KV] = grads[i, REST : REST + BLOCK]
        out[:, i * Q + KV : (i + 1) * Q] = grads[i, REST + BLOCK :]


def q_by_token(grads):
    return pl.pallas_call(
        q_by_token_kernel,
        out_shape=jax.ShapeDtypeStruct((BLOCK, KV_HEADS * Q), jnp.bfloat16),
        in_specs=[VMEM],
        out_specs=VMEM,
        cost_estimate=pl.CostEstimate(flops=0, transcendentals=0, bytes_accessed=2 * 2**20),
        compiler_params=SMALL,
        name="q_by_token",
    )(grads)


def kv_by_token_kernel(rest, low, grad_k, grad_v):
    for i in range(KV_HEADS):
        lanes = slice(i * HEAD_DIM, (i + 1) * HEAD_DIM)
        for ref, start in ((grad_k, 0), (grad_v, HEAD_DIM)):
            part = slice(start, start + HEAD_DIM)
            ref[:PROMPT, lanes] = low[i, :, part]
            ref[PROMPT:, lanes] = rest[i, :, part]


def kv_by_token(grads, low):
    out = jax.ShapeDtypeStruct((BLOCK, KV_HEADS * HEAD_DIM), jnp.bfloat16)
    whole = pl.BlockSpec(out.shape, lambda i: (0, 0))
    return pl.pallas_call(
        kv_by_token_kernel,
        grid=(1,),
        out_shape=(out, out),
        in_specs=[
            pl.BlockSpec((KV_HEADS, REST, KV), lambda i: (0, 0, 0)),
            pl.BlockSpec((KV_HEADS, PROMPT, KV), lambda i: (0, 0, 0)),
        ],
        out_specs=(whole, whole),
        cost_estimate=pl.CostEstimate(flops=0, transcendentals=0, bytes_accessed=2**20),
        compiler_params=SMALL,
        name="kv_by_token",
    )(grads, low)


def finish_kernel(partner, own, back, low, out):
    total = own[...] + back[partner_entry(partner)].astype(jnp.float32)
    out[0] = total.astype(out.dtype)
    for i in range(1, KV_HEADS):
        out[i] = low[i]


def finish(partner, own, back, low):
    return pl.pallas_call(
        finish_kernel,
        out_shape=jax.ShapeDtypeStruct(low.shape, jnp.bfloat16),
        in_specs=[SMEM, VMEM, VMEM, VMEM],
        out_specs=VMEM,
        cost_estimate=pl.CostEstimate(flops=0, transcendentals=0, bytes_accessed=2**18),
        compiler_params=SMALL,
        name="finish",
    )(partner, own, back, low)


def local(queries, keys, values, upstream, lengths, guests, advantage, partner):
    def swap(array):
        return lax.all_to_all(array, "head", split_axis=0, concat_axis=0, tiled=True)

    low = swap(lay_out(keys, values))
    packed = swap(pack(queries, keys, values))
    far = exchange(low[0], partner)
    grads, grads_low, far_grad, own = attention(
        partner, lengths, guests, advantage, packed, low, upstream, far
    )
    grads = swap(grads)
    grads_low = finish(partner, own, exchange(far_grad, partner), grads_low)
    grads_low, grads = lax.optimization_barrier((grads_low, grads))
    grads_low = swap(grads_low)
    return (q_by_token(grads),) + tuple(kv_by_token(grads, grads_low))


def solution(mesh):
    mesh = Mesh(mesh.devices.reshape(X, Z, CORE, KV_HEADS), TREES + ("head",))
    tokens = P(TREES + ("head",), None)
    trees = P(TREES, None)
    return jax.shard_map(
        local,
        mesh=mesh,
        in_specs=(tokens, tokens, tokens, P(TREES, "head"), trees, trees, trees, P()),
        out_specs=(tokens, tokens, tokens),
        check_vma=False,
    )
```

```python
import jax
import jax.numpy as jnp
from jax import lax
from jax.experimental import pallas as pl
from jax.experimental.pallas import tpu as pltpu
from jax.sharding import Mesh, PartitionSpec as P

HEAD_DIM = 128
PROMPT = 48
RESP = 8
RESP_LEN = 122
ROWS = 1024
GROUP = 4
KV_HEADS = 8
WINDOW = 128
Q = GROUP * HEAD_DIM
KV = 2 * HEAD_DIM
BLOCK = ROWS // KV_HEADS
REST = BLOCK - PROMPT
PACKED = REST + 2 * BLOCK
TREES = ("x", "z", "core")
PLANE = ("x", "core")
X, Z, CORE = 4, 12, 2


NT = (((1,), (1,)), ((), ()))
TN = (((0,), (0,)), ((), ()))
SCALING = HEAD_DIM ** (-0.5)
LOG2_E = 1.4426950408889634


def products(q_rows, keys, vals, cot):
    scores = lax.dot_general(keys, q_rows, NT, preferred_element_type=jnp.float32)
    grad_probs = lax.dot_general(vals, cot, NT, preferred_element_type=jnp.float32)
    return scores * (SCALING * LOG2_E), grad_probs


def backward(scores, grad_probs, q_rows, keys, cot):
    lifted = jnp.exp2(scores - jnp.max(scores, axis=0, keepdims=True))
    share = 1.0 / jnp.sum(lifted, axis=0, keepdims=True)
    inner = jnp.sum(lifted * grad_probs, axis=0, keepdims=True) * share
    probs = lifted * share
    grad_scores = (probs * (grad_probs - inner) * SCALING).astype(jnp.bfloat16)
    grad_v = jnp.dot(probs.astype(jnp.bfloat16), cot, preferred_element_type=jnp.float32)
    grad_k = jnp.dot(grad_scores, q_rows, preferred_element_type=jnp.float32)
    grad_q = lax.dot_general(grad_scores, keys, TN, preferred_element_type=jnp.float32)
    return grad_q, jnp.concatenate([grad_k, grad_v], axis=1)


def stack_heads(block):
    return jnp.concatenate(
        [block[:, j * HEAD_DIM : (j + 1) * HEAD_DIM] for j in range(GROUP)], axis=0
    )


def segments(start, rows):
    found, at = [], start
    while at < start + rows:
        block, first = divmod(at, BLOCK)
        last = min(PROMPT if first < PROMPT else BLOCK, first + start + rows - at)
        found.append((block, first, last, at - start))
        at += last - first
    return found


def q_index(block, first, last, head):
    shift = REST + head // 2 * BLOCK
    lanes = slice(head % 2 * HEAD_DIM, (head % 2 + 1) * HEAD_DIM)
    return block, slice(shift + first, shift + last), lanes


def kv_index(packed, low, block, first, last):
    if first < PROMPT:
        return low, (block, slice(first, last))
    return packed, (block, slice(first - PROMPT, last - PROMPT))


def attention_kernel(
    partner, lengths, guests, adv, packed, low, cot_ref, far_in, grads, grads_low, far_out, own_out, pre, acc, later
):
    iota = lax.broadcasted_iota
    pre[0] = low[0]
    pre[1] = far_in[partner_entry(partner)]
    acc[1] = jnp.zeros((PROMPT, KV), jnp.float32)
    causal = iota(jnp.int32, later.shape, 0) <= iota(jnp.int32, later.shape, 1)
    later[...] = jnp.where(causal, 0.0, -jnp.inf)

    def q_of(start, rows):
        return jnp.concatenate(
            [
                packed[q_index(block, first, last, head)]
                for head in range(GROUP)
                for block, first, last, _ in segments(start, rows)
            ],
            axis=0,
        )

    def kv_of(start, rows):
        parts = []
        for block, first, last, _ in segments(start, rows):
            ref, index = kv_index(packed, low, block, first, last)
            parts.append(ref[index])
        return parts

    def window(slot):
        first = PROMPT + RESP_LEN * slot
        start = first // 8 * 8
        return slice(start, start + WINDOW), first - start

    def load(slot):
        rows, skip = window(slot)
        guest = guests[0, slot]
        q_rows = q_of(rows.start, WINDOW)
        kv = jnp.concatenate([pre[guest]] + kv_of(rows.start, WINDOW), axis=0)
        keys, vals = kv[:, :HEAD_DIM], kv[:, HEAD_DIM:]
        token = iota(jnp.int32, (WINDOW, HEAD_DIM), 0) - skip
        weight = jnp.where((token >= 0) & (token < lengths[0, slot]), adv[0, slot], 0.0)
        cot = jnp.concatenate(
            [
                (cot_ref[rows, lanes].astype(jnp.float32) * weight).astype(jnp.bfloat16)
                for lanes in (slice(j * HEAD_DIM, (j + 1) * HEAD_DIM) for j in range(GROUP))
            ],
            axis=0,
        )
        return (q_rows, keys, cot), products(q_rows, keys, vals, cot)

    def emit(slot, operands, scores, grad_probs):
        rows, skip = window(slot)
        bias = later[...]
        if skip:
            top = jnp.where(iota(jnp.int32, (8, WINDOW), 0) < skip, -jnp.inf, bias[:8])
            bias = jnp.concatenate([top, bias[8:]], axis=0)
        bias = jnp.concatenate([bias] * GROUP, axis=1)
        scores = jnp.concatenate([scores[:PROMPT], scores[PROMPT:] + bias], axis=0)
        grad_q, grad_kv = backward(scores, grad_probs, *operands)
        acc[guests[0, slot]] += grad_kv[:PROMPT]
        for block, first, last, at in segments(rows.start, WINDOW):
            for head in range(GROUP):
                new = grad_q[head * WINDOW + at : head * WINDOW + at + last - first]
                store(grads, q_index(block, first, last, head), new, skip if at == 0 else 0)
            ref, index = kv_index(grads, grads_low, block, first, last)
            new = grad_kv[PROMPT + at : PROMPT + at + last - first]
            store(ref, index, new, skip if at == 0 else 0)

    def store(ref, index, new, skip):
        if skip:
            block, rows, *lanes = index
            old = ref[(block, slice(rows.start, rows.start + 8), *lanes)].astype(jnp.float32)
            top = jnp.where(iota(jnp.int32, old.shape, 0) < skip, old, new[:8])
            new = jnp.concatenate([top, new[8:]], axis=0) if new.shape[0] > 8 else top
        ref[index] = new.astype(jnp.bfloat16)

    q_rows = q_of(0, PROMPT)
    cot = stack_heads(cot_ref[:PROMPT, :])
    keys = pre[0, :, :HEAD_DIM]
    scores, grad_probs = products(q_rows, keys, pre[0, :, HEAD_DIM:], cot)
    query = iota(jnp.int32, scores.shape, 1)
    for j in range(1, GROUP):
        query = jnp.where(query >= PROMPT, query - PROMPT, query)
    scores = jnp.where(iota(jnp.int32, scores.shape, 0) <= query, scores, -jnp.inf)
    grad_q, acc[0] = backward(scores, grad_probs, q_rows, keys, cot)
    for head in range(GROUP):
        new = grad_q[head * PROMPT : (head + 1) * PROMPT]
        store(grads, q_index(0, 0, PROMPT, head), new, 0)

    ahead = load(0)
    for slot in range(RESP):
        operands, parts = ahead
        if slot + 1 < RESP:
            ahead = load(slot + 1)
        emit(slot, operands, *parts)
    own_out[...] = acc[0]
    grads_low[0] = acc[0].astype(jnp.bfloat16)
    far_out[...] = acc[1].astype(jnp.bfloat16)


VMEM = pl.BlockSpec(memory_space=pltpu.VMEM)
SMEM = pl.BlockSpec(memory_space=pltpu.SMEM)
SMALL = pltpu.CompilerParams(vmem_limit_bytes=8 * 2**20)
LARGE = pltpu.CompilerParams(vmem_limit_bytes=24 * 2**20)


def attention(partner, lengths, guests, adv, packed, low, cot, far):
    return pl.pallas_call(
        attention_kernel,
        out_shape=(
            jax.ShapeDtypeStruct(packed.shape, jnp.bfloat16),
            jax.ShapeDtypeStruct(low.shape, jnp.bfloat16),
            jax.ShapeDtypeStruct((PROMPT, KV), jnp.bfloat16),
            jax.ShapeDtypeStruct((PROMPT, KV), jnp.float32),
        ),
        in_specs=[SMEM] * 4 + [VMEM] * 4,
        out_specs=(VMEM,) * 4,
        scratch_shapes=[
            pltpu.VMEM((2, PROMPT, KV), jnp.bfloat16),
            pltpu.VMEM((2, PROMPT, KV), jnp.float32),
            pltpu.VMEM((WINDOW, WINDOW), jnp.float32),
        ],
        cost_estimate=pl.CostEstimate(flops=10**9, transcendentals=720896, bytes_accessed=5 * 2**20),
        compiler_params=LARGE,
        name="attention",
    )(partner, lengths, guests, adv, packed, low, cot, far)


def place():
    return tuple(lax.axis_index(name) for name in TREES)


def pick_kernel(partner, blocks, out):
    _, z, core = place()
    for i in range(X):
        wanted = partner[(i * Z + z) * CORE + core]
        out[i] = blocks[lax.rem(wanted, Z * CORE)]


def pick(partner, blocks):
    return pl.pallas_call(
        pick_kernel,
        out_shape=jax.ShapeDtypeStruct((X,) + blocks.shape[1:], blocks.dtype),
        in_specs=[SMEM, VMEM],
        out_specs=VMEM,
        cost_estimate=pl.CostEstimate(flops=0, transcendentals=0, bytes_accessed=2**18),
        compiler_params=SMALL,
        name="pick",
    )(partner, blocks)


def exchange(block, partner):
    wanted = pick(partner, lax.all_gather(block, ("z", "core")))
    return lax.all_gather(wanted, "x", axis=0, tiled=True)


def partner_entry(partner):
    x, z, core = place()
    return X * lax.div(partner[(x * Z + z) * CORE + core], Z * CORE) + x


def lay_out_kernel(keys, values, out):
    for i in range(KV_HEADS):
        lanes = slice(i * HEAD_DIM, (i + 1) * HEAD_DIM)
        out[i, :, :HEAD_DIM] = keys[:, lanes]
        out[i, :, HEAD_DIM:] = values[:, lanes]


def lay_out(keys, values):
    rows = pl.BlockSpec((PROMPT, KV_HEADS * HEAD_DIM), lambda i: (0, 0))
    return pl.pallas_call(
        lay_out_kernel,
        grid=(1,),
        out_shape=jax.ShapeDtypeStruct((KV_HEADS, PROMPT, KV), jnp.bfloat16),
        in_specs=[rows, rows],
        out_specs=pl.BlockSpec((KV_HEADS, PROMPT, KV), lambda i: (0, 0, 0)),
        cost_estimate=pl.CostEstimate(flops=0, transcendentals=0, bytes_accessed=2**19),
        name="lay_out",
    )(keys, values)


def pack_kernel(queries, keys, values, out):
    for i in range(KV_HEADS):
        lanes = slice(i * HEAD_DIM, (i + 1) * HEAD_DIM)
        out[i, :REST, :HEAD_DIM] = keys[PROMPT:, lanes]
        out[i, :REST, HEAD_DIM:] = values[PROMPT:, lanes]
        out[i, REST : REST + BLOCK] = queries[:, i * Q : i * Q + KV]
        out[i, REST + BLOCK :] = queries[:, i * Q + KV : (i + 1) * Q]


def pack(queries, keys, values):
    return pl.pallas_call(
        pack_kernel,
        out_shape=jax.ShapeDtypeStruct((KV_HEADS, PACKED, KV), jnp.bfloat16),
        in_specs=[VMEM] * 3,
        out_specs=VMEM,
        cost_estimate=pl.CostEstimate(flops=0, transcendentals=0, bytes_accessed=3 * 2**20),
        compiler_params=SMALL,
        name="pack",
    )(queries, keys, values)


def q_by_token_kernel(grads, out):
    for i in range(KV_HEADS):
        out[:, i * Q : i * Q + KV] = grads[i, REST : REST + BLOCK]
        out[:, i * Q + KV : (i + 1) * Q] = grads[i, REST + BLOCK :]


def q_by_token(grads):
    return pl.pallas_call(
        q_by_token_kernel,
        out_shape=jax.ShapeDtypeStruct((BLOCK, KV_HEADS * Q), jnp.bfloat16),
        in_specs=[VMEM],
        out_specs=VMEM,
        cost_estimate=pl.CostEstimate(flops=0, transcendentals=0, bytes_accessed=2 * 2**20),
        compiler_params=SMALL,
        name="q_by_token",
    )(grads)


def kv_by_token_kernel(rest, low, grad_k, grad_v):
    for i in range(KV_HEADS):
        lanes = slice(i * HEAD_DIM, (i + 1) * HEAD_DIM)
        for ref, start in ((grad_k, 0), (grad_v, HEAD_DIM)):
            part = slice(start, start + HEAD_DIM)
            ref[:PROMPT, lanes] = low[i, :, part]
            ref[PROMPT:, lanes] = rest[i, :, part]


def kv_by_token(grads, low):
    out = jax.ShapeDtypeStruct((BLOCK, KV_HEADS * HEAD_DIM), jnp.bfloat16)
    whole = pl.BlockSpec(out.shape, lambda i: (0, 0))
    return pl.pallas_call(
        kv_by_token_kernel,
        grid=(1,),
        out_shape=(out, out),
        in_specs=[
            pl.BlockSpec((KV_HEADS, REST, KV), lambda i: (0, 0, 0)),
            pl.BlockSpec((KV_HEADS, PROMPT, KV), lambda i: (0, 0, 0)),
        ],
        out_specs=(whole, whole),
        cost_estimate=pl.CostEstimate(flops=0, transcendentals=0, bytes_accessed=2**20),
        compiler_params=SMALL,
        name="kv_by_token",
    )(grads, low)


def finish_kernel(partner, own, back, low, out):
    total = own[...] + back[partner_entry(partner)].astype(jnp.float32)
    out[0] = total.astype(out.dtype)


def finish(partner, own, back, low):
    return pl.pallas_call(
        finish_kernel,
        grid=(1,),
        out_shape=jax.ShapeDtypeStruct(low.shape, jnp.bfloat16),
        in_specs=[SMEM, VMEM, VMEM, pl.BlockSpec(memory_space=pl.ANY)],
        out_specs=pl.BlockSpec((1, PROMPT, KV), lambda i: (0, 0, 0)),
        input_output_aliases={3: 0},
        cost_estimate=pl.CostEstimate(flops=0, transcendentals=0, bytes_accessed=2**17),
        compiler_params=SMALL,
        name="finish",
    )(partner, own, back, low)


def local(queries, keys, values, upstream, lengths, guests, advantage, partner):
    def swap(array):
        return lax.all_to_all(array, "head", split_axis=0, concat_axis=0, tiled=True)

    low = swap(lay_out(keys, values))
    packed = swap(pack(queries, keys, values))
    far = exchange(low[0], partner)
    grads, grads_low, far_grad, own = attention(
        partner, lengths, guests, advantage, packed, low, upstream, far
    )
    grads = swap(grads)
    grads_low = finish(partner, own, exchange(far_grad, partner), grads_low)
    grads_low, grads = lax.optimization_barrier((grads_low, grads))
    grads_low = swap(grads_low)
    return (q_by_token(grads),) + tuple(kv_by_token(grads, grads_low))


def solution(mesh):
    mesh = Mesh(mesh.devices.reshape(X, Z, CORE, KV_HEADS), TREES + ("head",))
    tokens = P(TREES + ("head",), None)
    trees = P(TREES, None)
    return jax.shard_map(
        local,
        mesh=mesh,
        in_specs=(tokens, tokens, tokens, P(TREES, "head"), trees, trees, trees, P()),
        out_specs=(tokens, tokens, tokens),
        check_vma=False,
    )
```
